32 devices in a mesh: row: 8 (over z, core), col: 4 (over y, x).
Axes of the slice: x: 2, y: 2, z: 4, core: 2. Of those that a mesh axis runs over, the one named last changes fastest.
Arguments:
- features: bfloat16 [8192, 256], P(('row', 'col')), may hold values from -6 to 6
- weight_in: bfloat16 [2, 256, 256], replicated, may hold values from -0.21875 to 0.21875
- weight_out: bfloat16 [2, 256, 256], replicated, may hold values from -0.21875 to 0.21875
- weight_self: bfloat16 [2, 256, 256], replicated, may hold values from -0.21875 to 0.21875
- layer_bias: float32 [2, 256], replicated, may hold values from -3 to 3
- out_degree: int32 [8192], P(('row', 'col')), may hold values from 1 to 64
- in_degree: int32 [8192], P(('row', 'col')), may hold values from 1 to 64
- tile_values: bfloat16 [4096, 128, 128], P(('row', 'col')), may hold values from 0 to 1
- tile_pick: int32 [4096], P(('row', 'col')), may hold values from 0 to 3
- tile_count: int32 [32], P(('row', 'col')), may hold values from 1 to 128, as said below
- cotangent: bfloat16 [8192, 256], P(('row', 'col')), may hold values from -6 to 6
Outputs:
- out_features: bfloat16 [8192, 256], P(('row', 'col'))
- grad_features: float32 [8192, 256], P(('row', 'col'))
- grad_weight_in: float32 [2, 256, 256], replicated
- grad_weight_out: float32 [2, 256, 256], replicated
- grad_weight_self: float32 [2, 256, 256], replicated
- grad_bias: float32 [2, 256], replicated
The draws below stay inside these ranges and needn't reach their ends.
Inputs may be any that keep to these rules, and one draw needn't show every extreme that they name: `tile_count`: slots at or above a device's count are empty and unused; in every draw some device has all 128 slots live. `tile_pick`: slot s of a device belongs to group s // (128 // 32), which fixes the node square of its tile as in the definition of A.
All inputs are finite; a program needn't handle non-finite values.
Results may differ from the reference program's by a relative error of at most 0.025.
Values may be sent and summed in bfloat16 or wider, within the bound.
A program may use at most 128 MiB of HBM per device.

```python
import jax
import jax.numpy as jnp
from jax import lax

F = 256
TILE = 128
TILES = 128
LAYERS = 2
NODES = 8192
BLK = 2
N_COL = 4
DEVICES = 32


def draw_tile_count(key, part):
    first_key, second_key = jax.random.split(jax.random.fold_in(key, 17))
    uniform_ints = jax.random.randint(first_key, (DEVICES,), 0, TILES, dtype=jnp.int32)
    counts = 1 + uniform_ints * uniform_ints // TILES
    fullest = jax.random.randint(second_key, (), 0, DEVICES, dtype=jnp.int32)
    device_ids = jnp.arange(DEVICES, dtype=jnp.int32)
    return jnp.where(device_ids == fullest, TILES, counts).astype(jnp.int32)


def plant(entries, rng, least, high):
    longest = entries.shape.index(max(entries.shape))
    spots = []
    for shift in (0, 1):
        where = [jax.random.randint(jax.random.fold_in(rng, axis), (), 0, length) for axis, length in enumerate(entries.shape)]
        where[longest] = (where[longest] + shift) % entries.shape[longest]
        spots.append(tuple(where))
    return entries.at[spots[0]].set(least).at[spots[1]].set(high)


def shard_levels(key, dims, cuts, least, high):
    factor_of = 1.0
    for position, shards_of in cuts:
        heights = jax.random.uniform(jax.random.fold_in(jax.random.fold_in(key, 6), position), (shards_of,), jnp.float32, least / len(cuts), high / len(cuts))
        factor_of = factor_of * jnp.repeat(jnp.exp(heights), dims[position] // shards_of).reshape((-1,) + (1,) * (len(dims) - 1 - position))
    return factor_of


def centred(key, dims, deviation, reach, cuts=(), kind=jnp.bfloat16):
    factor_of = shard_levels(key, dims, cuts, -0.22, 0.18) if cuts else 1.0
    array = jax.random.normal(key, dims, jnp.float32) * deviation * factor_of
    return jnp.minimum(jnp.maximum(array, -reach), reach).astype(kind)


def setup_inputs(seed: int = 0) -> dict:
    splits = jax.random.split(jax.random.key(seed), 12)
    features = centred(splits[0], (NODES, F), 1.0, 6.0, ((0, 32),))
    weight_in = centred(splits[1], (LAYERS, F, F), (3 * F) ** -0.5, 0.21875)
    weight_out = centred(splits[2], (LAYERS, F, F), (3 * F) ** -0.5, 0.21875)
    weight_self = centred(splits[3], (LAYERS, F, F), (3 * F) ** -0.5, 0.21875)
    layer_bias = centred(splits[4], (LAYERS, F), 0.5, 3.0, (), jnp.float32)
    out_degree = plant(jax.random.randint(splits[5], (NODES,), 1, 65), jax.random.fold_in(splits[5], 1), 1, 64).astype(jnp.int32)
    in_degree = plant(jax.random.randint(splits[6], (NODES,), 1, 65), jax.random.fold_in(splits[6], 1), 1, 64).astype(jnp.int32)
    tile_values = jnp.clip(1.0 * jax.random.uniform(splits[7], (DEVICES * TILES, TILE, TILE), jnp.float32) ** shard_levels(splits[7], (DEVICES * TILES, TILE, TILE), ((0, 32),), -0.2, 0.2), 0.0, 1.0).astype(jnp.bfloat16)
    tile_pick = plant(jax.random.randint(splits[8], (DEVICES * TILES,), 0, BLK * BLK), jax.random.fold_in(splits[8], 1), 0, (BLK * BLK) - 1).astype(jnp.int32)
    tile_count = draw_tile_count(jax.random.fold_in(splits[11], 71), 0)
    cotangent = centred(splits[10], (NODES, F), 1.0, 6.0, ((0, 32),))
    return {"features": features, "weight_in": weight_in, "weight_out": weight_out, "weight_self": weight_self, "layer_bias": layer_bias, "out_degree": out_degree, "in_degree": in_degree, "tile_values": tile_values, "tile_pick": tile_pick, "tile_count": tile_count, "cotangent": cotangent}


def activation(inputs):
    return jax.nn.gelu(inputs, approximate=True)

def sparse_product(operand, tile_values, tile_pick, tile_count, transposed):
    node_blocks = operand.reshape(NODES // TILE, TILE, F)
    per_peer = TILES // DEVICES
    slot_ids = jnp.arange(TILES, dtype=jnp.int32)
    dest_group = slot_ids // per_peer

    def add_device(running, device_id):
        tile_vals = lax.dynamic_slice_in_dim(tile_values, device_id * TILES, TILES, 0).astype(jnp.float32)
        tile_picks = lax.dynamic_slice_in_dim(tile_pick, device_id * TILES, TILES, 0)
        row_id = device_id // N_COL
        col_id = device_id % N_COL
        row_blocks = ((row_id * N_COL + dest_group % N_COL) * BLK + tile_picks // BLK).astype(jnp.int32)
        col_blocks = ((dest_group // N_COL * N_COL + col_id) * BLK + tile_picks % BLK).astype(jnp.int32)
        live_mask = slot_ids < tile_count[device_id]
        if transposed:
            from_blocks, to_blocks, einsum_form = (row_blocks, col_blocks, 'sji,sjf->sif')
        else:
            from_blocks, to_blocks, einsum_form = (col_blocks, row_blocks, 'sij,sjf->sif')
        gathered = jnp.take(node_blocks, from_blocks, axis=0).astype(jnp.float32)
        product = jnp.einsum(einsum_form, tile_vals, gathered, precision=lax.Precision.HIGHEST)
        product = jnp.where(live_mask[:, None, None], product, jnp.zeros_like(product))
        return (running.at[to_blocks].add(product), None)
    start_value = jnp.zeros((NODES // TILE, TILE, F), jnp.float32)
    running, unused = lax.scan(add_device, start_value, jnp.arange(DEVICES, dtype=jnp.int32))
    return running.reshape(NODES, F)

def reference(features, weight_in, weight_out, weight_self, layer_bias, out_degree, in_degree, tile_values, tile_pick, tile_count, cotangent):
    scale_in = (1.0 / jnp.sqrt(in_degree.astype(jnp.float32)))[:, None]
    scale_out = (1.0 / jnp.sqrt(out_degree.astype(jnp.float32)))[:, None]
    hidden = features
    stored = []
    for layer in range(LAYERS):
        scaled_in = (scale_in * hidden.astype(jnp.float32)).astype(jnp.bfloat16)
        scaled_out = (scale_out * hidden.astype(jnp.float32)).astype(jnp.bfloat16)
        msg_in = (scale_out * sparse_product(scaled_in, tile_values, tile_pick, tile_count, False)).astype(jnp.bfloat16)
        msg_out = (scale_in * sparse_product(scaled_out, tile_values, tile_pick, tile_count, True)).astype(jnp.bfloat16)
        preact = jnp.dot(msg_in, weight_in[layer], preferred_element_type=jnp.float32)
        preact = preact + jnp.dot(msg_out, weight_out[layer], preferred_element_type=jnp.float32)
        preact = preact + jnp.dot(hidden, weight_self[layer], preferred_element_type=jnp.float32)
        preact = preact + layer_bias[layer].astype(jnp.float32)[None, :]
        stored.append((hidden, msg_in, msg_out, preact))
        hidden = activation(preact).astype(jnp.bfloat16)
    out_features = hidden
    upstream = cotangent.astype(jnp.float32)
    grads_in, grads_out, grads_self, grads_bias = ([], [], [], [])
    for layer in reversed(range(LAYERS)):
        hidden, msg_in, msg_out, preact = stored[layer]
        unused, pullback = jax.vjp(activation, preact)
        grad_z = pullback(upstream)[0].astype(jnp.bfloat16)
        grads_in.append(jnp.dot(msg_in.T, grad_z, preferred_element_type=jnp.float32))
        grads_out.append(jnp.dot(msg_out.T, grad_z, preferred_element_type=jnp.float32))
        grads_self.append(jnp.dot(hidden.T, grad_z, preferred_element_type=jnp.float32))
        grads_bias.append(lax.optimization_barrier(jnp.sum(grad_z.astype(jnp.float32), axis=0)))
        back_in = (scale_out * jnp.dot(grad_z, weight_in[layer].T, preferred_element_type=jnp.float32)).astype(jnp.bfloat16)
        back_out = (scale_in * jnp.dot(grad_z, weight_out[layer].T, preferred_element_type=jnp.float32)).astype(jnp.bfloat16)
        upstream = scale_in * sparse_product(back_in, tile_values, tile_pick, tile_count, True)
        upstream = upstream + scale_out * sparse_product(back_out, tile_values, tile_pick, tile_count, False)
        upstream = upstream + jnp.dot(grad_z, weight_self[layer].T, preferred_element_type=jnp.float32)
    return (out_features, upstream, jnp.stack(grads_in[::-1]), jnp.stack(grads_out[::-1]), jnp.stack(grads_self[::-1]), jnp.stack(grads_bias[::-1]))
```

```python
import jax
import jax.numpy as jnp
from jax import lax
from jax.sharding import PartitionSpec as P


def activation(inputs):
    return jax.nn.gelu(inputs, approximate=True)


def dense_block(tile_values, tile_pick, tile_count, row_count, col_count, sub_blocks):
    tile_total, tile_size, unused = tile_values.shape
    per_peer = tile_total // (row_count * col_count)
    live = jnp.arange(tile_total, dtype=jnp.int32) < tile_count[0]
    picks = jnp.where(live, tile_pick, -1).reshape(row_count * col_count, per_peer)
    tiles = tile_values.reshape(row_count * col_count, per_peer, tile_size, tile_size)
    rows = []
    for row_half in range(sub_blocks):
        cols = []
        for col_half in range(sub_blocks):
            spot = row_half * sub_blocks + col_half
            total = 0.0
            for slot in range(per_peer):
                total = total + jnp.where(
                    (picks[:, slot] == spot)[:, None, None], tiles[:, slot].astype(jnp.float32), 0.0
                )
            cols.append(total.astype(jnp.bfloat16))
        rows.append(jnp.concatenate(cols, axis=2))
    squares = jnp.concatenate(rows, axis=1)
    side = sub_blocks * tile_size
    squares = squares.reshape(row_count, col_count, side, side)
    return squares.transpose(1, 2, 0, 3).reshape(col_count * side, row_count * side)


def per_device(
    features,
    weight_in,
    weight_out,
    weight_self,
    layer_bias,
    out_degree,
    in_degree,
    tile_values,
    tile_pick,
    tile_count,
    cotangent,
):
    row_count = lax.axis_size("row")
    col_count = lax.axis_size("col")
    sub_blocks = features.shape[0] // tile_values.shape[1]
    block = dense_block(tile_values, tile_pick, tile_count, row_count, col_count, sub_blocks)
    scale_in = 1.0 / jnp.sqrt(in_degree.astype(jnp.float32))
    scale_out = 1.0 / jnp.sqrt(out_degree.astype(jnp.float32))

    def forward_messages(first, second):
        row_rows = lax.all_gather(second, "col", axis=0, tiled=True)
        column_rows = lax.all_gather(first, "row", axis=0, tiled=True)
        reverse = lax.dot_general(
            block, row_rows, (((0,), (0,)), ((), ())), preferred_element_type=jnp.float32
        )
        direct = jnp.dot(block, column_rows, preferred_element_type=jnp.float32)
        summed_reverse = lax.psum_scatter(reverse, "row", scatter_dimension=0, tiled=True)
        summed_direct = lax.psum_scatter(direct, "col", scatter_dimension=0, tiled=True)
        return (summed_direct, summed_reverse)

    layer_total = weight_in.shape[0]
    hidden = features
    stored = []
    for layer in range(layer_total):
        hidden_wide = hidden.astype(jnp.float32)
        scaled_in = (scale_in[:, None] * hidden_wide).astype(jnp.bfloat16)
        scaled_out = (scale_out[:, None] * hidden_wide).astype(jnp.bfloat16)
        summed_direct, summed_reverse = forward_messages(scaled_in, scaled_out)
        msg_in = (scale_out[:, None] * summed_direct).astype(jnp.bfloat16)
        msg_out = (scale_in[:, None] * summed_reverse).astype(jnp.bfloat16)
        preact = jnp.dot(msg_in, weight_in[layer], preferred_element_type=jnp.float32)
        preact = preact + jnp.dot(msg_out, weight_out[layer], preferred_element_type=jnp.float32)
        preact = preact + jnp.dot(hidden, weight_self[layer], preferred_element_type=jnp.float32)
        preact = preact + layer_bias[layer][None, :]
        stored.append((hidden, msg_in, msg_out, preact))
        hidden = activation(preact).astype(jnp.bfloat16)
    out_features = hidden
    upstream = cotangent.astype(jnp.float32)
    ones = jnp.ones((features.shape[0], 8), jnp.bfloat16)
    grads = []
    for layer in reversed(range(layer_total)):
        hidden, msg_in, msg_out, preact = stored[layer]
        unused, pullback = jax.vjp(activation, preact)
        grad_z = pullback(upstream)[0].astype(jnp.bfloat16)
        parts = jnp.concatenate([msg_in, msg_out, hidden, ones], axis=1)
        grads.append(jnp.einsum("nf,ng->fg", parts, grad_z, preferred_element_type=jnp.float32))
        back_in = (
            scale_out[:, None]
            * jnp.dot(grad_z, weight_in[layer].T, preferred_element_type=jnp.float32)
        ).astype(jnp.bfloat16)
        back_out = (
            scale_in[:, None]
            * jnp.dot(grad_z, weight_out[layer].T, preferred_element_type=jnp.float32)
        ).astype(jnp.bfloat16)
        backward_summed_direct, backward_summed_reverse = forward_messages(back_out, back_in)
        upstream = (
            scale_out[:, None] * backward_summed_direct
            + scale_in[:, None] * backward_summed_reverse
        )
        upstream = upstream + jnp.dot(
            grad_z, weight_self[layer].T, preferred_element_type=jnp.float32
        )
    total = lax.psum(jnp.stack(grads[::-1]), ("row", "col"))
    width = features.shape[1]
    return (
        out_features,
        upstream,
        total[:, :width],
        total[:, width : 2 * width],
        total[:, 2 * width : 3 * width],
        total[:, 3 * width],
    )


def solution(mesh):
    return jax.shard_map(
        per_device,
        mesh=mesh,
        in_specs=(
            P(("row", "col"), None),
            P(),
            P(),
            P(),
            P(),
            P(("row", "col")),
            P(("row", "col")),
            P(("row", "col"), None, None),
            P(("row", "col")),
            P(("row", "col")),
            P(("row", "col"), None),
        ),
        out_specs=(P(("row", "col"), None), P(("row", "col"), None), P(), P(), P(), P()),
        check_vma=False,
    )
```

```python
import jax
import jax.numpy as jnp
from jax import lax
from jax.sharding import PartitionSpec as P


def activation(inputs):
    return jax.nn.gelu(inputs, approximate=True)


def dense_block(tile_values, tile_pick, tile_count, row_count, col_count, sub_blocks):
    tile_total, tile_size, unused = tile_values.shape
    per_peer = tile_total // (row_count * col_count)
    live = jnp.arange(tile_total, dtype=jnp.int32) < tile_count[0]
    picks = jnp.where(live, tile_pick, -1).reshape(row_count * col_count, per_peer)
    tiles = tile_values.reshape(row_count * col_count, per_peer, tile_size, tile_size)
    rows = []
    for row_half in range(sub_blocks):
        cols = []
        for col_half in range(sub_blocks):
            spot = row_half * sub_blocks + col_half
            total = 0.0
            for slot in range(per_peer):
                total = total + jnp.where(
                    (picks[:, slot] == spot)[:, None, None], tiles[:, slot].astype(jnp.float32), 0.0
                )
            cols.append(total.astype(jnp.bfloat16))
        rows.append(jnp.concatenate(cols, axis=2))
    squares = jnp.concatenate(rows, axis=1)
    side = sub_blocks * tile_size
    squares = squares.reshape(row_count, col_count, side, side)
    return squares.transpose(1, 2, 0, 3).reshape(col_count * side, row_count * side)


def per_device(
    features,
    weight_in,
    weight_out,
    weight_self,
    layer_bias,
    out_degree,
    in_degree,
    tile_values,
    tile_pick,
    tile_count,
    cotangent,
):
    row_count = lax.axis_size("row")
    col_count = lax.axis_size("col")
    sub_blocks = features.shape[0] // tile_values.shape[1]
    block = dense_block(tile_values, tile_pick, tile_count, row_count, col_count, sub_blocks)
    scale_in = 1.0 / jnp.sqrt(in_degree.astype(jnp.float32))
    scale_out = 1.0 / jnp.sqrt(out_degree.astype(jnp.float32))

    def forward_messages(first, second):
        row_rows = lax.all_gather(second, "col", axis=0, tiled=True)
        column_rows = lax.all_gather(first, "row", axis=0, tiled=True)
        reverse = lax.dot_general(
            block, row_rows, (((0,), (0,)), ((), ())), preferred_element_type=jnp.float32
        )
        direct = jnp.dot(block, column_rows, preferred_element_type=jnp.float32)
        summed_reverse = lax.psum_scatter(reverse, "row", scatter_dimension=0, tiled=True)
        pieces = direct.astype(jnp.bfloat16).reshape((lax.axis_size("col"), -1, direct.shape[1]))
        pieces = lax.all_to_all(pieces, "col", 0, 0, tiled=True)
        summed_direct = jnp.sum(pieces.astype(jnp.float32), axis=0)
        return (summed_direct, summed_reverse)

    layer_total = weight_in.shape[0]
    hidden = features
    stored = []
    for layer in range(layer_total):
        hidden_wide = hidden.astype(jnp.float32)
        scaled_in = (scale_in[:, None] * hidden_wide).astype(jnp.bfloat16)
        scaled_out = (scale_out[:, None] * hidden_wide).astype(jnp.bfloat16)
        summed_direct, summed_reverse = forward_messages(scaled_in, scaled_out)
        msg_in = (scale_out[:, None] * summed_direct).astype(jnp.bfloat16)
        msg_out = (scale_in[:, None] * summed_reverse).astype(jnp.bfloat16)
        preact = jnp.dot(msg_in, weight_in[layer], preferred_element_type=jnp.float32)
        preact = preact + jnp.dot(msg_out, weight_out[layer], preferred_element_type=jnp.float32)
        preact = preact + jnp.dot(hidden, weight_self[layer], preferred_element_type=jnp.float32)
        preact = preact + layer_bias[layer][None, :]
        stored.append((hidden, msg_in, msg_out, preact))
        hidden = activation(preact).astype(jnp.bfloat16)
    out_features = hidden
    upstream = cotangent.astype(jnp.float32)
    ones = jnp.ones((features.shape[0], 256), jnp.bfloat16)
    grads = []
    for layer in reversed(range(layer_total)):
        hidden, msg_in, msg_out, preact = stored[layer]
        unused, pullback = jax.vjp(activation, preact)
        grad_z = pullback(upstream)[0].astype(jnp.bfloat16)
        parts = jnp.concatenate([msg_in, msg_out, hidden, ones], axis=1)
        grads.append(jnp.einsum("nf,ng->fg", parts, grad_z, preferred_element_type=jnp.float32))
        back_in = (
            scale_out[:, None]
            * jnp.dot(grad_z, weight_in[layer].T, preferred_element_type=jnp.float32)
        ).astype(jnp.bfloat16)
        back_out = (
            scale_in[:, None]
            * jnp.dot(grad_z, weight_out[layer].T, preferred_element_type=jnp.float32)
        ).astype(jnp.bfloat16)
        backward_summed_direct, backward_summed_reverse = forward_messages(back_out, back_in)
        upstream = (
            scale_out[:, None] * backward_summed_direct
            + scale_in[:, None] * backward_summed_reverse
        )
        upstream = upstream + jnp.dot(
            grad_z, weight_self[layer].T, preferred_element_type=jnp.float32
        )
    width = features.shape[1]
    total = jnp.concatenate(grads[::-1], axis=0)
    total = lax.psum_scatter(total, "row", scatter_dimension=0, tiled=True)
    total = lax.psum_scatter(total, "col", scatter_dimension=0, tiled=True)
    total = lax.all_gather(total, ("row", "col"), axis=0, tiled=True)
    total = total.reshape(layer_total, -1, width)
    return (
        out_features,
        upstream,
        total[:, :width],
        total[:, width : 2 * width],
        total[:, 2 * width : 3 * width],
        total[:, 3 * width],
    )


def solution(mesh):
    return jax.shard_map(
        per_device,
        mesh=mesh,
        in_specs=(
            P(("row", "col"), None),
            P(),
            P(),
            P(),
            P(),
            P(("row", "col")),
            P(("row", "col")),
            P(("row", "col"), None, None),
            P(("row", "col")),
            P(("row", "col")),
            P(("row", "col"), None),
        ),
        out_specs=(P(("row", "col"), None), P(("row", "col"), None), P(), P(), P(), P()),
        check_vma=False,
    )
```
